32 devices in a mesh: frame: 4 (over z), space: 8 (over y, x, core).
Axes of the slice: x: 2, y: 2, z: 4, core: 2. Of those that a mesh axis runs over, the one named last changes fastest.
Arguments:
- latents: bfloat16 [2, 4, 512, 3072], P(None, 'frame', 'space'), may hold values from -6 to 6
- target: bfloat16 [2, 4, 512, 3072], P(None, 'frame', 'space'), may hold values from -6 to 6
- timesteps: int32 [2], replicated, may hold values from 0 to 999
- valid: int32 [2, 2], replicated, may hold values from 1 to 16, as said below
- tile_mask: int32 [2, 16, 16], replicated, may hold values from 0 to 1, as said below
- w_mod: bfloat16 [256, 18432], replicated, may hold values from -0.5 to 0.5
- w_sqkv: bfloat16 [3, 3072, 2048], P(None, None, 'space'), may hold values from -0.109375 to 0.109375
- w_sout: bfloat16 [2048, 3072], P('space'), may hold values from -0.125 to 0.125
- w_tqkv: bfloat16 [3, 3072, 2048], P(None, None, 'frame'), may hold values from -0.109375 to 0.109375
- w_tout: bfloat16 [2048, 3072], P('frame'), may hold values from -0.125 to 0.125
Outputs:
- mixed: bfloat16 [2, 4, 512, 3072], P(None, 'frame', 'space')
- loss: float32 [], replicated
The draws below stay inside these ranges and needn't reach their ends.
Inputs may be any that keep to these rules, and one draw needn't show every extreme that they name: Each video's valid frame count is 1 to 4 and valid tile count 1 to 16; video 0 is whole. `tile_mask`: entries are 0 or 1, with ones on the diagonal of every video's mask.
All inputs are finite; a program needn't handle non-finite values.
Results may differ from the reference program's by a relative error of at most 0.017.
Values may be sent and summed in bfloat16 or wider, within the bound.
A program may use at most 128 MiB of HBM per device.

```python
import math
import jax
import jax.numpy as jnp
from jax import lax

D = 3072
HEADS = 16
HEAD_DIM = 128
FREQ = 256
TILE = 32
VIDEOS = 2
SPD = 64
FRAMES = 4
SPAN = 512
TILES = 16
N_FRAME = 4
N_SPACE = 8


def draw_valid(key, part):
    counts = jax.random.randint(jax.random.fold_in(key, 11), (VIDEOS,), 1, FRAMES + 1)
    tiles = jax.random.randint(jax.random.fold_in(key, 12), (VIDEOS,), 1, TILES + 1)
    counts = counts.at[0].set(FRAMES)
    tiles = tiles.at[0].set(TILES)
    return jnp.stack([counts, tiles], 1).astype(jnp.int32)


def draw_tile_mask(key, part):
    bits = jax.random.randint(jax.random.fold_in(key, 21), (VIDEOS, TILES, TILES), 0, 2)
    diagonal = jnp.eye(TILES, dtype=jnp.int32)
    return jnp.maximum(bits, diagonal[None]).astype(jnp.int32)


def steps_of(own_key, extent, cuts, smallest, high):
    level = 1.0
    for dim, blocks in cuts:
        heights = jax.random.uniform(jax.random.fold_in(jax.random.fold_in(own_key, 6), dim), (blocks,), jnp.float32, smallest / len(cuts), high / len(cuts))
        level = level * jnp.repeat(jnp.exp(heights), extent[dim] // blocks).reshape((-1,) + (1,) * (len(extent) - 1 - dim))
    return level


def gaussian(own_key, shape, spread, reach, shards=(), kind=jnp.bfloat16):
    drawn = jax.random.normal(own_key, shape, jnp.float32) * spread
    if len(shards) > 0:
        drawn = steps_of(own_key, shape, shards, -0.22, 0.18) * drawn
    return jnp.clip(drawn, min=-reach, max=reach).astype(kind)


def setup_inputs(seed: int = 0) -> dict:
    arg_keys = jax.random.split(jax.random.key(seed), 11)
    latents = gaussian(arg_keys[0], (VIDEOS, FRAMES, SPAN, D), 1.0, 6.0, ((1, 4), (2, 8)))
    target = gaussian(arg_keys[1], (VIDEOS, FRAMES, SPAN, D), 1.0, 6.0, ((1, 4), (2, 8)))
    timesteps = jax.random.randint(arg_keys[2], (VIDEOS,), 0, 1000).astype(jnp.int32)
    valid = draw_valid(jax.random.fold_in(arg_keys[10], 71), 0)
    tile_mask = draw_tile_mask(jax.random.fold_in(arg_keys[10], 71), 0)
    w_mod = gaussian(arg_keys[5], (FREQ, 6 * D), (FREQ // 2) ** -0.5, 0.5)
    w_sqkv = gaussian(arg_keys[6], (3, D, HEADS * HEAD_DIM), D ** -0.5, 0.109375, ((2, 8),))
    w_sout = gaussian(arg_keys[7], (HEADS * HEAD_DIM, D), (HEADS * HEAD_DIM) ** -0.5, 0.125, ((0, 8),))
    w_tqkv = gaussian(arg_keys[8], (3, D, HEADS * HEAD_DIM), D ** -0.5, 0.109375, ((2, 4),))
    w_tout = gaussian(arg_keys[9], (HEADS * HEAD_DIM, D), (HEADS * HEAD_DIM) ** -0.5, 0.125, ((0, 4),))
    return {"latents": latents, "target": target, "timesteps": timesteps, "valid": valid, "tile_mask": tile_mask, "w_mod": w_mod, "w_sqkv": w_sqkv, "w_sout": w_sout, "w_tqkv": w_tqkv, "w_tout": w_tout}


def layer_norm(values):
    mean = lax.optimization_barrier(jnp.mean(values, -1, keepdims=True))
    centred = values - mean
    var = lax.optimization_barrier(jnp.mean(centred * centred, -1, keepdims=True))
    return centred * lax.rsqrt(var + 1e-06)

def time_embed(timesteps):
    half = FREQ // 2
    freqs = jnp.exp(-math.log(10000.0) * jnp.arange(half, dtype=jnp.float32) / half)
    angles = timesteps.astype(jnp.float32)[:, None] * freqs[None, :]
    return jnp.concatenate([jnp.cos(angles), jnp.sin(angles)], -1).astype(jnp.bfloat16)

def frame_attention(qkv, count, tiles, heads):
    length = qkv.shape[0]
    cols = heads * HEAD_DIM
    scale = 1.0 / math.sqrt(HEAD_DIM)
    query = jnp.transpose(qkv[:, :cols].reshape(length, heads, HEAD_DIM), (1, 0, 2))
    keys = jnp.transpose(qkv[:, cols:2 * cols].reshape(length, heads, HEAD_DIM), (1, 0, 2))
    values = jnp.transpose(qkv[:, 2 * cols:].reshape(length, heads, HEAD_DIM), (1, 0, 2))
    tile_ids = jnp.arange(length, dtype=jnp.int32) // TILE
    expanded = jnp.repeat(jnp.repeat(tiles, TILE, axis=0), TILE, axis=1)
    allowed = (expanded == 1) & (tile_ids[None, :] < count) | (tile_ids[:, None] == tile_ids[None, :])

    def one_head(parts):
        q_head, k_head, v_head = parts
        scores = jnp.dot(q_head.astype(jnp.float32), k_head.astype(jnp.float32).T) * scale
        scores = jnp.where(allowed, scores, -1e+30)
        top = lax.optimization_barrier(jnp.max(scores, -1, keepdims=True))
        weights = jnp.exp(scores - top)
        probs = (weights / lax.optimization_barrier(jnp.sum(weights, -1, keepdims=True))).astype(jnp.bfloat16)
        return jnp.dot(probs, v_head, preferred_element_type=jnp.float32).astype(jnp.bfloat16)
    outs = lax.map(one_head, (query, keys, values))
    return jnp.transpose(outs, (1, 0, 2)).reshape(length, cols)

def temporal_attention(qkv, count, heads):
    frames, places = (qkv.shape[0], qkv.shape[1])
    cols = heads * HEAD_DIM
    scale = 1.0 / math.sqrt(HEAD_DIM)
    query = qkv[..., :cols].reshape(frames, places, heads, HEAD_DIM).astype(jnp.float32)
    keys = qkv[..., cols:2 * cols].reshape(frames, places, heads, HEAD_DIM).astype(jnp.float32)
    values = qkv[..., 2 * cols:].reshape(frames, places, heads, HEAD_DIM).astype(jnp.float32)
    scores = jnp.einsum('fphd,gphd->phfg', query, keys) * scale
    frame_ids = jnp.arange(frames, dtype=jnp.int32)
    allowed = (frame_ids[None, :] < count) | (frame_ids[:, None] == frame_ids[None, :])
    scores = jnp.where(allowed, scores, -1e+30)
    top = lax.optimization_barrier(jnp.max(scores, -1, keepdims=True))
    weights = jnp.exp(scores - top)
    probs = (weights / lax.optimization_barrier(jnp.sum(weights, -1, keepdims=True))).astype(jnp.bfloat16)
    outs = jnp.einsum('phfg,gphd->fphd', probs.astype(jnp.float32), values).astype(jnp.bfloat16)
    return outs.reshape(frames, places, cols)

def group_project(attended, w_out, groups):
    rows = attended.shape[0]
    width = w_out.shape[1]
    parts = attended.reshape(rows, groups, -1).astype(jnp.float32)
    weights = w_out.reshape(groups, -1, width).astype(jnp.float32)
    terms = jnp.einsum('rgc,gcd->rgd', parts, weights).astype(jnp.bfloat16)
    return lax.optimization_barrier(jnp.sum(terms.astype(jnp.float32), axis=1))

def modulate(values, shift, scale):
    return (layer_norm(values.astype(jnp.float32)) * (1.0 + scale[:, None, None, :]) + shift[:, None, None, :]).astype(jnp.bfloat16)

def reference(latents, target, timesteps, valid, tile_mask, w_mod, w_sqkv, w_sout, w_tqkv, w_tout):
    videos, frames, span, width = latents.shape
    embed = time_embed(timesteps)
    mod = jnp.dot(embed, w_mod, preferred_element_type=jnp.float32)
    shift_one, scale_one, gate_one, shift_two, scale_two, gate_two = jnp.split(mod, 6, axis=1)
    h_one = modulate(latents, shift_one, scale_one)
    w_flat = jnp.concatenate([w_sqkv[0], w_sqkv[1], w_sqkv[2]], axis=1)
    tokens = h_one.reshape(videos * frames, span, width)
    tile_counts = jnp.repeat(valid[:, 1], frames)
    tiles = jnp.repeat(tile_mask, frames, axis=0)

    def per_frame(parts):
        frame_tokens, count, tiles_one = parts
        qkv = jnp.dot(frame_tokens, w_flat, preferred_element_type=jnp.float32).astype(jnp.bfloat16)
        attended = frame_attention(qkv, count, tiles_one, HEADS)
        return group_project(attended, w_sout, N_SPACE)
    spatial = lax.map(per_frame, (tokens, tile_counts, tiles)).reshape(videos, frames, span, width)
    x_one = (latents.astype(jnp.float32) + gate_one[:, None, None, :] * spatial).astype(jnp.bfloat16)
    h_two = modulate(x_one, shift_two, scale_two)
    blocks = span // SPD
    w_tflat = jnp.concatenate([w_tqkv[0], w_tqkv[1], w_tqkv[2]], axis=1)
    columns = h_two.reshape(videos, frames, blocks, SPD, width).transpose(0, 2, 1, 3, 4).reshape(videos * blocks, frames, SPD, width)
    frame_counts = jnp.repeat(valid[:, 0], blocks)

    def per_block(parts):
        block_tokens, count = parts
        qkv = jnp.dot(block_tokens, w_tflat, preferred_element_type=jnp.float32).astype(jnp.bfloat16)
        attended = temporal_attention(qkv, count, HEADS)
        projected = group_project(attended.reshape(frames * SPD, -1), w_tout, N_FRAME)
        return projected.reshape(frames, SPD, width)
    temporal = lax.map(per_block, (columns, frame_counts))
    temporal = temporal.reshape(videos, blocks, frames, SPD, width).transpose(0, 2, 1, 3, 4).reshape(videos, frames, span, width)
    mixed = (x_one.astype(jnp.float32) + gate_two[:, None, None, :] * temporal).astype(jnp.bfloat16)
    diff = mixed.astype(jnp.float32) - target.astype(jnp.float32)
    squares = lax.optimization_barrier(jnp.mean(diff * diff, -1))
    frame_ids = jnp.arange(frames, dtype=jnp.int32)
    tile_ids = jnp.arange(span, dtype=jnp.int32) // TILE
    mask = (frame_ids[None, :, None] < valid[:, 0][:, None, None]) & (tile_ids[None, None, :] < valid[:, 1][:, None, None])
    count = jnp.sum(valid[:, 0] * valid[:, 1]).astype(jnp.float32) * TILE
    loss = jnp.sum(jnp.where(mask, squares, 0.0)) / count
    return (mixed, loss)
```

```python
import functools
import math

import jax
import jax.numpy as jnp
from jax import lax
from jax.experimental import pallas as pl
from jax.experimental.pallas import tpu as pltpu
from jax.sharding import PartitionSpec as P

HEAD_DIM = 128
FREQ = 256
TILE = 32
PAD = 128
MESH = pl.DeviceIdType.MESH


def time_embed(timesteps):
    half = FREQ // 2
    freqs = jnp.exp(-math.log(10000.0) * jnp.arange(half, dtype=jnp.float32) / half)
    angles = timesteps.astype(jnp.float32)[:, None] * freqs[None, :]
    return jnp.concatenate([jnp.cos(angles), jnp.sin(angles)], -1).astype(jnp.bfloat16)


def norm_mod(values, shift, scale):
    mean = jnp.mean(values, -1, keepdims=True)
    centred = values - mean
    var = jnp.mean(centred * centred, -1, keepdims=True)
    return (centred * lax.rsqrt(var + 1e-06) * (1.0 + scale) + shift).astype(jnp.bfloat16)


def attend(query, keys, values, allowed):
    scores = lax.dot_general(
        query, keys, (((1,), (1,)), ((), ())), preferred_element_type=jnp.float32
    ) * (1.0 / math.sqrt(HEAD_DIM))
    scores = jnp.where(allowed, scores, -1e30)
    top = jnp.max(scores, -1, keepdims=True)
    weights = jnp.exp(scores - top)
    probs = (weights * (1.0 / jnp.sum(weights, -1, keepdims=True))).astype(jnp.bfloat16)
    return jnp.dot(probs, values, preferred_element_type=jnp.float32).astype(jnp.bfloat16)


def expand(table, ids):
    rows = jnp.dot(ids, table, preferred_element_type=jnp.float32).astype(jnp.bfloat16)
    return lax.dot_general(rows, ids, (((1,), (1,)), ((), ())), preferred_element_type=jnp.float32)


def kernel(
    n_space, n_frame, offsets, nx, ny,
    lat_ref, mod_ref, tiles_ref, framesok_ref, wq_hbm, wso_hbm, wt_hbm,
    x1_ref, att_ref,
    G, PR, R, H, C, wq, wso, wt, qkv, att, tqkv, A, smask, tmask,
    ag_s, ag_r, fw_s, fw_r, pr_s, pr_r, rs_s, rs_r, z_s, z_r, a_s, a_r, w_sem,
):
    V, L, D = lat_ref.shape
    nch = n_space // 2
    span = n_space * L
    sp = lax.axis_index("space")
    fr = lax.axis_index("frame")
    core = sp % 2
    chip = sp // 2
    cx, cy = chip % nx, chip // nx
    no = len(offsets)

    def plus(k):
        dx, dy = offsets[k]
        return ((cy + dy) % ny) * nx + (cx + dx) % nx

    def minus(k):
        dx, dy = offsets[k]
        return ((cy + ny - dy) % ny) * nx + (cx + nx - dx) % nx

    sib = {"space": chip * 2 + (1 - core)}

    loads = [
        pltpu.make_async_copy(wq_hbm, wq, w_sem.at[0]),
        pltpu.make_async_copy(wso_hbm, wso, w_sem.at[1]),
        pltpu.make_async_copy(wt_hbm, wt, w_sem.at[2]),
    ]
    for ld in loads:
        ld.start()

    bar = pltpu.get_barrier_semaphore()
    for k in range(1, no):
        pl.semaphore_signal(bar, inc=1, device_id={"space": plus(k) * 2 + core}, device_id_type=MESH)
    pl.semaphore_signal(bar, inc=1, device_id=sib, device_id_type=MESH)
    for o in range(1, n_frame):
        pl.semaphore_signal(bar, inc=1, device_id={"frame": (fr + o) % n_frame}, device_id_type=MESH)

    def rcopy(src, dst, s, r, dev):
        return pltpu.make_async_remote_copy(
            src_ref=src, dst_ref=dst, send_sem=s, recv_sem=r, device_id=dev, device_id_type=MESH
        )

    def ag(v, k):
        return rcopy(
            G.at[v, chip, core], G.at[v, chip, core], ag_s.at[v, k], ag_r.at[v, k],
            {"space": plus(k) * 2 + core},
        )

    def ag_in(v, k):
        slot = G.at[v, minus(k), core]
        return rcopy(slot, slot, ag_s.at[v, k], ag_r.at[v, k], {"space": plus(k) * 2 + core})

    def fw(v, k):
        slot = G.at[v, minus(k), core]
        return rcopy(slot, slot, fw_s.at[v, k], fw_r.at[v, k], sib)

    def fw_in(v, k):
        slot = G.at[v, minus(k), 1 - core]
        return rcopy(slot, slot, fw_s.at[v, k], fw_r.at[v, k], sib)

    def pr(v, k):
        return rcopy(G.at[v, plus(k), 1 - core], PR.at[v, k], pr_s.at[v, k], pr_r.at[v, k], sib)

    def rs(v, k):
        return rcopy(
            G.at[v, plus(k), core], R.at[v, k], rs_s.at[v, k], rs_r.at[v, k],
            {"space": plus(k) * 2 + core},
        )

    def zg(v, o):
        return rcopy(
            H.at[v, fr], H.at[v, fr], z_s.at[v, o], z_r.at[v, o], {"frame": (fr + o) % n_frame}
        )

    def zg_in(v, o):
        slot = H.at[v, (fr + n_frame - o) % n_frame]
        return rcopy(slot, slot, z_s.at[v, o], z_r.at[v, o], {"frame": (fr + o) % n_frame})

    tc = tqkv.shape[2]

    def ax(v, o):
        cols = pl.ds(pl.multiple_of(fr * tc, tc), tc)
        dst = (fr + o) % n_frame
        return rcopy(
            A.at[v, dst], C.at[v, :, cols], a_s.at[v, o], a_r.at[v, o], {"frame": dst}
        )

    def ax_in(v, o):
        src = (fr + n_frame - o) % n_frame
        cols = pl.ds(pl.multiple_of(src * tc, tc), tc)
        return rcopy(
            A.at[v, src], C.at[v, :, cols], a_s.at[v, o], a_r.at[v, o], {"frame": src}
        )

    def mod(v, i):
        return mod_ref[v, i : i + 1, :]

    for v in range(V):
        G[v, chip, core] = norm_mod(lat_ref[v].astype(jnp.float32), mod(v, 0), mod(v, 1))
        if v == 0:
            pl.semaphore_wait(bar, (no - 1) + 1 + (n_frame - 1))
        for k in range(no - 1, 0, -1):
            ag(v, k).start()
        fw(v, 0).start()

    row = lax.broadcasted_iota(jnp.int32, (span, PAD), 0) // TILE
    col = lax.broadcasted_iota(jnp.int32, (span, PAD), 1)
    tile_ids = (row == col).astype(jnp.bfloat16)
    tl = n_frame * L
    rowf = lax.broadcasted_iota(jnp.int32, (tl, PAD), 0) // L
    colf = lax.broadcasted_iota(jnp.int32, (tl, PAD), 1)
    frame_ids = (rowf == colf).astype(jnp.bfloat16)
    place_q = lax.broadcasted_iota(jnp.int32, (tl, tl), 0) % L
    place_k = lax.broadcasted_iota(jnp.int32, (tl, tl), 1) % L
    for v in range(V):
        smask[v] = expand(tiles_ref[v], tile_ids).astype(jnp.bfloat16)
        both = jnp.where(place_q == place_k, expand(framesok_ref[v], frame_ids), 0.0)
        tmask[v] = both.astype(jnp.bfloat16)

    def forward(v):
        for k in range(1, no):
            ag_in(v, k).wait_recv()
            fw(v, k).start()

    sc = qkv.shape[2]
    QB = 256

    def spatial(v):
        for k in range(no):
            fw_in(v, k).wait_recv()
        if v == 0:
            loads[0].wait()
        mt = 256 // (2 * L)
        nm = nch // mt

        def qkv_step(i, _):
            j, m = i // nm, i % nm
            x = G[v, pl.ds(m * mt, mt)].reshape(256, D)
            qkv[j, pl.ds(pl.multiple_of(m * 256, 256), 256), :] = jnp.dot(
                x, wq[j], preferred_element_type=jnp.float32
            ).astype(jnp.bfloat16)
            return 0

        lax.fori_loop(0, 3 * nm, qkv_step, 0)

        for h in range(sc // HEAD_DIM):
            hs = slice(h * HEAD_DIM, (h + 1) * HEAD_DIM)

            def att_step(i, _):
                rows = pl.ds(pl.multiple_of(i * QB, QB), QB)
                ok = smask[v, rows, :].astype(jnp.float32) > 0.5
                att[rows, hs] = attend(qkv[0, rows, hs], qkv[1, :, hs], qkv[2, :, hs], ok)
                return 0

            lax.fori_loop(0, span // QB, att_step, 0)

        for k in range(1, no):
            ag(v, k).wait_send()
        for k in range(no):
            fw(v, k).wait_send()
        if v == 0:
            loads[1].wait()

        CB = 512

        def term_step(i, _):
            cols = pl.ds(pl.multiple_of(i * CB, CB), CB)
            t = jnp.dot(att[...], wso[:, cols], preferred_element_type=jnp.float32)
            G[v, :, :, :, cols] = t.astype(jnp.bfloat16).reshape(nch, 2, L, CB)
            return 0

        lax.fori_loop(0, D // CB, term_step, 0)
        for k in range(no - 1, -1, -1):
            pr(v, k).start()

    def reduce_send(v):
        for k in range(no - 1, 0, -1):
            pr(v, k).wait_recv()
            c = plus(k)
            G[v, c, core] = (
                G[v, c, core].astype(jnp.float32) + PR[v, k].astype(jnp.float32)
            ).astype(jnp.bfloat16)
            rs(v, k).start()

    def finish_spatial(v):
        pr(v, 0).wait_recv()
        so = G[v, chip, core].astype(jnp.float32) + PR[v, 0].astype(jnp.float32)
        for k in range(1, no):
            rs(v, k).wait_recv()
            so = so + R[v, k].astype(jnp.float32)
        x1 = (lat_ref[v].astype(jnp.float32) + mod(v, 2) * so).astype(jnp.bfloat16)
        x1_ref[v] = x1
        H[v, fr] = norm_mod(x1.astype(jnp.float32), mod(v, 3), mod(v, 4))
        for o in range(1, n_frame):
            zg(v, o).start()

    def temporal(v):
        for o in range(1, n_frame):
            zg_in(v, o).wait_recv()
        if v == 0:
            loads[2].wait()
        NB = 256
        nn = tc // NB

        def tqkv_step(i, _):
            j, n = i // nn, i % nn
            cols = pl.ds(pl.multiple_of(n * NB, NB), NB)
            tqkv[j, :, cols] = jnp.dot(
                H[v].reshape(tl, D), wt[j, :, cols], preferred_element_type=jnp.float32
            ).astype(jnp.bfloat16)
            return 0

        lax.fori_loop(0, 3 * nn, tqkv_step, 0)
        ok = tmask[v].astype(jnp.float32) > 0.5
        for h in range(tc // HEAD_DIM):
            hs = slice(h * HEAD_DIM, (h + 1) * HEAD_DIM)
            out = attend(tqkv[0, :, hs], tqkv[1, :, hs], tqkv[2, :, hs], ok)
            A[v, :, :, hs] = out.reshape(n_frame, L, HEAD_DIM)
        for o in range(1, n_frame):
            ax(v, o).start()
        C[v, :, pl.ds(pl.multiple_of(fr * tc, tc), tc)] = A[v, fr]

    forward(0)
    spatial(0)
    reduce_send(0)
    forward(1)
    spatial(1)
    reduce_send(1)
    finish_spatial(0)
    finish_spatial(1)
    temporal(0)
    temporal(1)
    for v in range(V):
        for o in range(1, n_frame):
            ax_in(v, o).wait_recv()
        att_ref[v] = C[v]
    for v in range(V):
        for k in range(no):
            pr(v, k).wait_send()
        for k in range(1, no):
            rs(v, k).wait_send()
        for o in range(1, n_frame):
            zg(v, o).wait_send()
            ax(v, o).wait_send()


def run_kernel(latents, mod, tiles, frames_ok, w_sqkv, w_sout, w_tqkv):
    V, L, D = latents.shape
    n_space = lax.axis_size("space")
    n_frame = lax.axis_size("frame")
    nch = n_space // 2
    ny = 2 if nch % 2 == 0 else 1
    nx = nch // ny
    offsets = [(dx, dy) for dy in range(ny) for dx in range(nx)]
    no = len(offsets)
    sc, tc = w_sqkv.shape[2], w_tqkv.shape[2]
    span = n_space * L
    tl = n_frame * L
    bf = jnp.bfloat16
    dma = pltpu.SemaphoreType.DMA
    vm = pl.BlockSpec(memory_space=pltpu.VMEM)
    hbm = pl.BlockSpec(memory_space=pl.ANY)
    return pl.pallas_call(
        functools.partial(kernel, n_space, n_frame, offsets, nx, ny),
        out_shape=(
            jax.ShapeDtypeStruct((V, L, D), bf),
            jax.ShapeDtypeStruct((V, L, n_frame * tc), bf),
        ),
        in_specs=[vm, vm, vm, vm, hbm, hbm, hbm],
        out_specs=(vm, vm),
        scratch_shapes=[
            pltpu.VMEM((V, nch, 2, L, D), bf),
            pltpu.VMEM((V, no, L, D), bf),
            pltpu.VMEM((V, no, L, D), bf),
            pltpu.VMEM((V, n_frame, L, D), bf),
            pltpu.VMEM((V, L, n_frame * tc), bf),
            pltpu.VMEM(w_sqkv.shape, bf),
            pltpu.VMEM(w_sout.shape, bf),
            pltpu.VMEM(w_tqkv.shape, bf),
            pltpu.VMEM((3, span, sc), bf),
            pltpu.VMEM((span, sc), bf),
            pltpu.VMEM((3, tl, tc), bf),
            pltpu.VMEM((V, n_frame, L, tc), bf),
            pltpu.VMEM((V, span, span), bf),
            pltpu.VMEM((V, tl, tl), bf),
            dma((V, no)), dma((V, no)), dma((V, no)), dma((V, no)),
            dma((V, no)), dma((V, no)), dma((V, no)), dma((V, no)),
            dma((V, n_frame)), dma((V, n_frame)), dma((V, n_frame)), dma((V, n_frame)),
            dma((3,)),
        ],
        compiler_params=pltpu.CompilerParams(
            collective_id=0, has_side_effects=True, vmem_limit_bytes=60 * 1024 * 1024
        ),
        cost_estimate=pl.CostEstimate(
            flops=20_000_000_000, bytes_accessed=300_000_000, transcendentals=3_000_000
        ),
        name="block",
    )(latents, mod, tiles, frames_ok, w_sqkv, w_sout, w_tqkv)


def shards(latents, target, timesteps, valid, tile_mask, w_mod, w_sqkv, w_sout, w_tqkv, w_tout):
    videos, frames_dev, span_dev, width = latents.shape
    n_frame = lax.axis_size("frame")
    w_tall = lax.all_gather(w_tout, "frame", axis=0, tiled=True)
    embed = time_embed(timesteps)
    mod = jnp.dot(embed, w_mod, preferred_element_type=jnp.float32).reshape(videos, 6, width)
    nt = tile_mask.shape[1]
    t_ids = jnp.arange(nt, dtype=jnp.int32)
    tiles = ((tile_mask == 1) & (t_ids[None, None, :] < valid[:, 1][:, None, None])) | (
        t_ids[None, :, None] == t_ids[None, None, :]
    )
    tiles = jnp.pad(tiles.astype(jnp.bfloat16), ((0, 0), (0, PAD - nt), (0, PAD - nt)))
    p_ids = jnp.arange(PAD, dtype=jnp.int32)
    frames_ok = (
        (p_ids[None, None, :] < valid[:, 0][:, None, None])
        | (p_ids[None, :, None] == p_ids[None, None, :])
    ).astype(jnp.bfloat16)
    x_one, own = run_kernel(
        latents.reshape(videos, span_dev, width), mod, tiles, frames_ok, w_sqkv, w_sout, w_tqkv
    )
    temporal = jnp.dot(
        own.reshape(videos * span_dev, -1), w_tall, preferred_element_type=jnp.float32
    ).reshape(videos, span_dev, width)
    mixed = (x_one.astype(jnp.float32) + mod[:, 5][:, None, :] * temporal).astype(jnp.bfloat16)
    diff = mixed.astype(jnp.float32) - target.reshape(videos, span_dev, width).astype(jnp.float32)
    squares = jnp.mean(diff * diff, -1)
    frame_id = lax.axis_index("frame")
    tile_ids = (lax.axis_index("space") * span_dev + jnp.arange(span_dev, dtype=jnp.int32)) // TILE
    mask = (frame_id < valid[:, 0][:, None]) & (tile_ids[None, :] < valid[:, 1][:, None])
    total = lax.psum(jnp.sum(jnp.where(mask, squares, 0.0)), ("frame", "space"))
    count = jnp.sum(valid[:, 0] * valid[:, 1]).astype(jnp.float32) * TILE
    return (mixed.reshape(latents.shape), total / count)


def solution(mesh):
    return jax.shard_map(
        shards,
        mesh=mesh,
        in_specs=(
            P(None, "frame", "space", None),
            P(None, "frame", "space", None),
            P(),
            P(),
            P(),
            P(),
            P(None, None, "space"),
            P("space", None),
            P(None, None, "frame"),
            P("frame", None),
        ),
        out_specs=(P(None, "frame", "space", None), P()),
        check_vma=False,
    )
```

```python
import functools
import math

import jax
import jax.numpy as jnp
from jax import lax
from jax.experimental import pallas as pl
from jax.experimental.pallas import tpu as pltpu
from jax.sharding import PartitionSpec as P

HEAD_DIM = 128
FREQ = 256
TILE = 32
PAD = 128
MESH = pl.DeviceIdType.MESH


def time_embed(timesteps):
    half = FREQ // 2
    freqs = jnp.exp(-math.log(10000.0) * jnp.arange(half, dtype=jnp.float32) / half)
    angles = timesteps.astype(jnp.float32)[:, None] * freqs[None, :]
    return jnp.concatenate([jnp.cos(angles), jnp.sin(angles)], -1).astype(jnp.bfloat16)


def norm_mod(values, shift, scale):
    mean = jnp.mean(values, -1, keepdims=True)
    centred = values - mean
    var = jnp.mean(centred * centred, -1, keepdims=True)
    return (centred * lax.rsqrt(var + 1e-06) * (1.0 + scale) + shift).astype(jnp.bfloat16)


def attend(query, keys, values, allowed):
    scores = lax.dot_general(
        query, keys, (((1,), (1,)), ((), ())), preferred_element_type=jnp.float32
    ) * (1.0 / math.sqrt(HEAD_DIM))
    scores = jnp.where(allowed, scores, -1e30)
    top = jnp.max(scores, -1, keepdims=True)
    weights = jnp.exp(scores - top)
    probs = (weights * (1.0 / jnp.sum(weights, -1, keepdims=True))).astype(jnp.bfloat16)
    return jnp.dot(probs, values, preferred_element_type=jnp.float32).astype(jnp.bfloat16)


def expand(table, ids):
    rows = jnp.dot(ids, table, preferred_element_type=jnp.float32).astype(jnp.bfloat16)
    return lax.dot_general(rows, ids, (((1,), (1,)), ((), ())), preferred_element_type=jnp.float32)


def kernel(
    n_space, n_frame, offsets, nx, ny,
    lat_ref, mod_ref, tiles_ref, framesok_ref, tokw_ref, wq_hbm, wso_hbm, wt_hbm, wto_hbm, tgt_hbm,
    mixed_ref, loss_ref, W,
    G, PR, R, H, C, x1_ref, tgt, LS, LF, wq, wso, wt, qkv, att, tqkv, A, smask, tmask,
    ag_s, ag_r, fw_s, fw_r, pr_s, pr_r, rs_s, rs_r, z_s, z_r, a_s, a_r,
    wz_s, wz_r, wp_s, wp_r, ws_s, ws_r, l_s, l_r, lf_s, lf_r, w_sem, wl_sem,
):
    V, L, D = lat_ref.shape
    nch = n_space // 2
    span = n_space * L
    sp = lax.axis_index("space")
    fr = lax.axis_index("frame")
    core = sp % 2
    chip = sp // 2
    cx, cy = chip % nx, chip // nx
    no = len(offsets)

    def plus(k):
        dx, dy = offsets[k]
        return ((cy + dy) % ny) * nx + (cx + dx) % nx

    def minus(k):
        dx, dy = offsets[k]
        return ((cy + ny - dy) % ny) * nx + (cx + nx - dx) % nx

    FR = wto_hbm.shape[0]
    U = FR // n_space

    def frame_rows(f):
        return pl.ds(pl.multiple_of(f * FR, FR), FR)

    def unit(f, s):
        return W.at[pl.ds(pl.multiple_of(f * FR + s * U, U), U)]

    sib = {"space": chip * 2 + (1 - core)}

    loads = [
        pltpu.make_async_copy(wq_hbm, wq, w_sem.at[0]),
        pltpu.make_async_copy(wso_hbm, wso, w_sem.at[1]),
        pltpu.make_async_copy(wt_hbm, wt, w_sem.at[2]),
        pltpu.make_async_copy(tgt_hbm, tgt, w_sem.at[3]),
        pltpu.make_async_copy(wto_hbm, W.at[frame_rows(fr)], w_sem.at[4]),
    ]
    for ld in loads:
        ld.start()

    bar = pltpu.get_barrier_semaphore()
    for o in range(1, n_space):
        pl.semaphore_signal(bar, inc=1, device_id={"space": (sp + o) % n_space}, device_id_type=MESH)
    for o in range(1, n_frame):
        pl.semaphore_signal(bar, inc=1, device_id={"frame": (fr + o) % n_frame}, device_id_type=MESH)

    def rcopy(src, dst, s, r, dev):
        return pltpu.make_async_remote_copy(
            src_ref=src, dst_ref=dst, send_sem=s, recv_sem=r, device_id=dev, device_id_type=MESH
        )

    def ag(v, k):
        return rcopy(
            G.at[v, chip, core], G.at[v, chip, core], ag_s.at[v, k], ag_r.at[v, k],
            {"space": plus(k) * 2 + core},
        )

    def ag_in(v, k):
        slot = G.at[v, minus(k), core]
        return rcopy(slot, slot, ag_s.at[v, k], ag_r.at[v, k], {"space": plus(k) * 2 + core})

    def fw(v, k):
        slot = G.at[v, minus(k), core]
        return rcopy(slot, slot, fw_s.at[v, k], fw_r.at[v, k], sib)

    def fw_in(v, k):
        slot = G.at[v, minus(k), 1 - core]
        return rcopy(slot, slot, fw_s.at[v, k], fw_r.at[v, k], sib)

    def pr(v, k):
        return rcopy(G.at[v, plus(k), 1 - core], PR.at[v, k], pr_s.at[v, k], pr_r.at[v, k], sib)

    def rs(v, k):
        return rcopy(
            G.at[v, plus(k), core], R.at[v, k], rs_s.at[v, k], rs_r.at[v, k],
            {"space": plus(k) * 2 + core},
        )

    def zg(v, o):
        return rcopy(
            H.at[v, fr], H.at[v, fr], z_s.at[v, o], z_r.at[v, o], {"frame": (fr + o) % n_frame}
        )

    def zg_in(v, o):
        slot = H.at[v, (fr + n_frame - o) % n_frame]
        return rcopy(slot, slot, z_s.at[v, o], z_r.at[v, o], {"frame": (fr + o) % n_frame})

    tc = tqkv.shape[2]

    def ax(v, o):
        cols = pl.ds(pl.multiple_of(fr * tc, tc), tc)
        dst = (fr + o) % n_frame
        return rcopy(
            A.at[v, dst], C.at[v, :, cols], a_s.at[v, o], a_r.at[v, o], {"frame": dst}
        )

    def ax_in(v, o):
        src = (fr + n_frame - o) % n_frame
        cols = pl.ds(pl.multiple_of(src * tc, tc), tc)
        return rcopy(
            A.at[v, src], C.at[v, :, cols], a_s.at[v, o], a_r.at[v, o], {"frame": src}
        )

    def wz(o):
        src = wto_hbm.at[pl.ds(pl.multiple_of(sp * U, U), U)]
        return rcopy(
            src, unit(fr, sp), wz_s.at[o], wz_r.at[o], {"frame": (fr + o) % n_frame}
        )

    def wz_in(o):
        slot = unit((fr + n_frame - o) % n_frame, sp)
        return rcopy(slot, slot, wz_s.at[o], wz_r.at[o], {"frame": (fr + o) % n_frame})

    def wp(o, k):
        slot = unit((fr + n_frame - o) % n_frame, sp)
        return rcopy(slot, slot, wp_s.at[o, k], wp_r.at[o, k], {"space": plus(k) * 2 + core})

    def wp_in(o, k):
        slot = unit((fr + n_frame - o) % n_frame, minus(k) * 2 + core)
        return rcopy(slot, slot, wp_s.at[o, k], wp_r.at[o, k], {"space": plus(k) * 2 + core})

    def ws(o, k):
        slot = unit((fr + n_frame - o) % n_frame, minus(k) * 2 + core)
        return rcopy(slot, slot, ws_s.at[o, k], ws_r.at[o, k], sib)

    def ws_in(o, k):
        slot = unit((fr + n_frame - o) % n_frame, minus(k) * 2 + 1 - core)
        return rcopy(slot, slot, ws_s.at[o, k], ws_r.at[o, k], sib)

    def ls(o):
        return rcopy(
            LS.at[sp], LS.at[sp], l_s.at[o], l_r.at[o], {"space": (sp + o) % n_space}
        )

    def ls_in(o):
        slot = LS.at[(sp + n_space - o) % n_space]
        return rcopy(slot, slot, l_s.at[o], l_r.at[o], {"space": (sp + o) % n_space})

    def lf(o):
        return rcopy(
            LF.at[fr], LF.at[fr], lf_s.at[o], lf_r.at[o], {"frame": (fr + o) % n_frame}
        )

    def lf_in(o):
        slot = LF.at[(fr + n_frame - o) % n_frame]
        return rcopy(slot, slot, lf_s.at[o], lf_r.at[o], {"frame": (fr + o) % n_frame})

    def mod(v, i):
        return mod_ref[v, i : i + 1, :]

    for v in range(V):
        G[v, chip, core] = norm_mod(lat_ref[v].astype(jnp.float32), mod(v, 0), mod(v, 1))
        if v == 0:
            pl.semaphore_wait(bar, (n_space - 1) + (n_frame - 1))
        for k in range(no - 1, 0, -1):
            ag(v, k).start()
        fw(v, 0).start()
    for o in range(1, n_frame):
        wz(o).start()

    row = lax.broadcasted_iota(jnp.int32, (span, PAD), 0) // TILE
    col = lax.broadcasted_iota(jnp.int32, (span, PAD), 1)
    tile_ids = (row == col).astype(jnp.bfloat16)
    tl = n_frame * L
    rowf = lax.broadcasted_iota(jnp.int32, (tl, PAD), 0) // L
    colf = lax.broadcasted_iota(jnp.int32, (tl, PAD), 1)
    frame_ids = (rowf == colf).astype(jnp.bfloat16)
    place_q = lax.broadcasted_iota(jnp.int32, (tl, tl), 0) % L
    place_k = lax.broadcasted_iota(jnp.int32, (tl, tl), 1) % L
    for v in range(V):
        smask[v] = expand(tiles_ref[v], tile_ids).astype(jnp.bfloat16)
        both = jnp.where(place_q == place_k, expand(framesok_ref[v], frame_ids), 0.0)
        tmask[v] = both.astype(jnp.bfloat16)

    def forward(v):
        for k in range(1, no):
            ag_in(v, k).wait_recv()
            fw(v, k).start()

    sc = qkv.shape[2]
    QB = 256

    def spatial(v):
        for k in range(no):
            fw_in(v, k).wait_recv()
        if v == 0:
            loads[0].wait()
        mt = 256 // (2 * L)
        nm = nch // mt

        def qkv_step(i, _):
            j, m = i // nm, i % nm
            x = G[v, pl.ds(m * mt, mt)].reshape(256, D)
            qkv[j, pl.ds(pl.multiple_of(m * 256, 256), 256), :] = jnp.dot(
                x, wq[j], preferred_element_type=jnp.float32
            ).astype(jnp.bfloat16)
            return 0

        lax.fori_loop(0, 3 * nm, qkv_step, 0)

        for h in range(sc // HEAD_DIM):
            hs = slice(h * HEAD_DIM, (h + 1) * HEAD_DIM)

            def att_step(i, _):
                rows = pl.ds(pl.multiple_of(i * QB, QB), QB)
                ok = smask[v, rows, :].astype(jnp.float32) > 0.5
                att[rows, hs] = attend(qkv[0, rows, hs], qkv[1, :, hs], qkv[2, :, hs], ok)
                return 0

            lax.fori_loop(0, span // QB, att_step, 0)

        for k in range(1, no):
            ag(v, k).wait_send()
        for k in range(no):
            fw(v, k).wait_send()
        if v == 0:
            loads[1].wait()

        CB = 512

        def term_step(i, _):
            cols = pl.ds(pl.multiple_of(i * CB, CB), CB)
            t = jnp.dot(att[...], wso[:, cols], preferred_element_type=jnp.float32)
            G[v, :, :, :, cols] = t.astype(jnp.bfloat16).reshape(nch, 2, L, CB)
            return 0

        lax.fori_loop(0, D // CB, term_step, 0)
        for k in range(no - 1, -1, -1):
            pr(v, k).start()

    def reduce_send(v):
        for k in range(no - 1, 0, -1):
            pr(v, k).wait_recv()
            c = plus(k)
            G[v, c, core] = (
                G[v, c, core].astype(jnp.float32) + PR[v, k].astype(jnp.float32)
            ).astype(jnp.bfloat16)
            rs(v, k).start()

    def finish_spatial(v):
        pr(v, 0).wait_recv()
        so = G[v, chip, core].astype(jnp.float32) + PR[v, 0].astype(jnp.float32)
        for k in range(1, no):
            rs(v, k).wait_recv()
            so = so + R[v, k].astype(jnp.float32)
        x1 = (lat_ref[v].astype(jnp.float32) + mod(v, 2) * so).astype(jnp.bfloat16)
        x1_ref[v] = x1
        H[v, fr] = norm_mod(x1.astype(jnp.float32), mod(v, 3), mod(v, 4))
        for o in range(1, n_frame):
            zg(v, o).start()

    def temporal(v):
        for o in range(1, n_frame):
            zg_in(v, o).wait_recv()
        if v == 0:
            loads[2].wait()
        NB = 256
        nn = tc // NB

        def tqkv_step(i, _):
            j, n = i // nn, i % nn
            cols = pl.ds(pl.multiple_of(n * NB, NB), NB)
            tqkv[j, :, cols] = jnp.dot(
                H[v].reshape(tl, D), wt[j, :, cols], preferred_element_type=jnp.float32
            ).astype(jnp.bfloat16)
            return 0

        lax.fori_loop(0, 3 * nn, tqkv_step, 0)
        ok = tmask[v].astype(jnp.float32) > 0.5
        for h in range(tc // HEAD_DIM):
            hs = slice(h * HEAD_DIM, (h + 1) * HEAD_DIM)
            out = attend(tqkv[0, :, hs], tqkv[1, :, hs], tqkv[2, :, hs], ok)
            A[v, :, :, hs] = out.reshape(n_frame, L, HEAD_DIM)
        for o in range(1, n_frame):
            ax(v, o).start()
        C[v, :, pl.ds(pl.multiple_of(fr * tc, tc), tc)] = A[v, fr]

    forward(0)
    spatial(0)
    reduce_send(0)
    forward(1)
    spatial(1)
    reduce_send(1)
    finish_spatial(0)
    finish_spatial(1)
    for o in range(1, n_frame):
        wz_in(o).wait_recv()
        for k in range(no - 1, 0, -1):
            wp(o, k).start()
        ws(o, 0).start()
    temporal(0)
    for o in range(1, n_frame):
        for k in range(1, no):
            wp_in(o, k).wait_recv()
            ws(o, k).start()
    temporal(1)

    for v in range(V):
        for k in range(no):
            pr(v, k).wait_send()
        for k in range(1, no):
            rs(v, k).wait_send()
    for o in range(1, n_frame):
        for k in range(no):
            ws_in(o, k).wait_recv()
    loads[4].wait()
    rows = FR * n_frame
    slots = [G.at[v, c, e] for v in range(V) for c in range(nch) for e in range(2)]
    slots += [PR.at[v, k] for v in range(V) for k in range(no)]
    slots += [R.at[v, k] for v in range(V) for k in range(no)]
    pulls = [
        pltpu.make_async_copy(W.at[pl.ds(b * L, L)], slots[b], wl_sem.at[b])
        for b in range(rows // L)
    ]
    for p in pulls:
        p.start()
    quads = [(G, v, c) for v in range(V) for c in range(0, nch, 2)]
    quads += [(PR, v, k) for v in range(V) for k in range(0, no, 4)]
    quads += [(R, v, k) for v in range(V) for k in range(0, no, 4)]
    quads = quads[: rows // (4 * L)]
    for v in range(V):
        for o in range(1, n_frame):
            ax_in(v, o).wait_recv()
    loads[3].wait()
    for p in pulls:
        p.wait()
    CB = 512

    def out_step(i, total):
        cols = pl.ds(pl.multiple_of(i * CB, CB), CB)
        acc = jnp.zeros((V * L, CB), jnp.float32)
        for q, (buf, v, c) in enumerate(quads):
            if buf is G:
                w = buf[v, c : c + 2, :, :, cols].reshape(4 * L, CB)
            else:
                w = buf[v, c : c + 4, :, cols].reshape(4 * L, CB)
            a = C[:, :, q * 4 * L : (q + 1) * 4 * L].reshape(V * L, 4 * L)
            acc = acc + jnp.dot(a, w, preferred_element_type=jnp.float32)
        part = []
        for v in range(V):
            gate = mod_ref[v, 5:6, cols]
            m = x1_ref[v, :, cols].astype(jnp.float32) + gate * acc[v * L : (v + 1) * L]
            m = m.astype(jnp.bfloat16)
            mixed_ref[v, :, cols] = m
            diff = m.astype(jnp.float32) - tgt[v, :, cols].astype(jnp.float32)
            part.append(jnp.sum(diff * diff, -1, keepdims=True))
        return total + jnp.concatenate(part, 0)

    squares = lax.fori_loop(0, D // CB, out_step, jnp.zeros((V * L, 1), jnp.float32)) * (1.0 / D)
    kept = squares.reshape(V, L, 1) * tokw_ref[...]
    LS[sp] = jnp.broadcast_to(jnp.sum(jnp.sum(kept, 0), 0, keepdims=True), (8, 128))
    for o in range(1, n_space):
        ls(o).start()
    for o in range(1, n_space):
        ls_in(o).wait_recv()
    LF[fr] = jnp.sum(LS[...], 0)
    for o in range(1, n_frame):
        lf(o).start()
    for o in range(1, n_frame):
        lf_in(o).wait_recv()
    loss_ref[...] = jnp.sum(LF[...], 0)

    for v in range(V):
        for o in range(1, n_frame):
            zg(v, o).wait_send()
            ax(v, o).wait_send()
    for o in range(1, n_frame):
        wz(o).wait_send()
        lf(o).wait_send()
        for k in range(no):
            ws(o, k).wait_send()
        for k in range(1, no):
            wp(o, k).wait_send()
    for o in range(1, n_space):
        ls(o).wait_send()


def run_kernel(latents, mod, tiles, frames_ok, tokw, w_sqkv, w_sout, w_tqkv, w_tout, target):
    V, L, D = latents.shape
    n_space = lax.axis_size("space")
    n_frame = lax.axis_size("frame")
    nch = n_space // 2
    ny = 2 if nch % 2 == 0 else 1
    nx = nch // ny
    offsets = [(dx, dy) for dy in range(ny) for dx in range(nx)]
    no = len(offsets)
    sc, tc = w_sqkv.shape[2], w_tqkv.shape[2]
    span = n_space * L
    tl = n_frame * L
    bf = jnp.bfloat16
    dma = pltpu.SemaphoreType.DMA
    vm = pl.BlockSpec(memory_space=pltpu.VMEM)
    hbm = pl.BlockSpec(memory_space=pl.ANY)
    return pl.pallas_call(
        functools.partial(kernel, n_space, n_frame, offsets, nx, ny),
        out_shape=(
            jax.ShapeDtypeStruct((V, L, D), bf),
            jax.ShapeDtypeStruct((8, 128), jnp.float32),
            jax.ShapeDtypeStruct((n_frame * w_tout.shape[0], D), bf),
        ),
        in_specs=[vm, vm, vm, vm, vm, hbm, hbm, hbm, hbm, hbm],
        out_specs=(vm, vm, hbm),
        scratch_shapes=[
            pltpu.VMEM((V, nch, 2, L, D), bf),
            pltpu.VMEM((V, no, L, D), bf),
            pltpu.VMEM((V, no, L, D), bf),
            pltpu.VMEM((V, n_frame, L, D), bf),
            pltpu.VMEM((V, L, n_frame * tc), bf),
            pltpu.VMEM((V, L, D), bf),
            pltpu.VMEM((V, L, D), bf),
            pltpu.VMEM((n_space, 8, 128), jnp.float32),
            pltpu.VMEM((n_frame, 8, 128), jnp.float32),
            pltpu.VMEM(w_sqkv.shape, bf),
            pltpu.VMEM(w_sout.shape, bf),
            pltpu.VMEM(w_tqkv.shape, bf),
            pltpu.VMEM((3, span, sc), bf),
            pltpu.VMEM((span, sc), bf),
            pltpu.VMEM((3, tl, tc), bf),
            pltpu.VMEM((V, n_frame, L, tc), bf),
            pltpu.VMEM((V, span, span), bf),
            pltpu.VMEM((V, tl, tl), bf),
            dma((V, no)), dma((V, no)), dma((V, no)), dma((V, no)),
            dma((V, no)), dma((V, no)), dma((V, no)), dma((V, no)),
            dma((V, n_frame)), dma((V, n_frame)), dma((V, n_frame)), dma((V, n_frame)),
            dma((n_frame,)), dma((n_frame,)), dma((n_frame, no)), dma((n_frame, no)),
            dma((n_frame, no)), dma((n_frame, no)), dma((n_space,)), dma((n_space,)),
            dma((n_frame,)), dma((n_frame,)), dma((5,)), dma((n_frame * w_tout.shape[0] // L,)),
        ],
        compiler_params=pltpu.CompilerParams(
            collective_id=0, has_side_effects=True, vmem_limit_bytes=60 * 1024 * 1024
        ),
        cost_estimate=pl.CostEstimate(
            flops=20_000_000_000, bytes_accessed=300_000_000, transcendentals=3_000_000
        ),
        name="block",
    )(latents, mod, tiles, frames_ok, tokw, w_sqkv, w_sout, w_tqkv, w_tout, target)


def shards(latents, target, timesteps, valid, tile_mask, w_mod, w_sqkv, w_sout, w_tqkv, w_tout):
    videos, frames_dev, span_dev, width = latents.shape
    embed = time_embed(timesteps)
    mod = jnp.dot(embed, w_mod, preferred_element_type=jnp.float32).reshape(videos, 6, width)
    nt = tile_mask.shape[1]
    t_ids = jnp.arange(nt, dtype=jnp.int32)
    tiles = ((tile_mask == 1) & (t_ids[None, None, :] < valid[:, 1][:, None, None])) | (
        t_ids[None, :, None] == t_ids[None, None, :]
    )
    tiles = jnp.pad(tiles.astype(jnp.bfloat16), ((0, 0), (0, PAD - nt), (0, PAD - nt)))
    p_ids = jnp.arange(PAD, dtype=jnp.int32)
    frames_ok = (
        (p_ids[None, None, :] < valid[:, 0][:, None, None])
        | (p_ids[None, :, None] == p_ids[None, None, :])
    ).astype(jnp.bfloat16)
    tile_ids = (lax.axis_index("space") * span_dev + jnp.arange(span_dev, dtype=jnp.int32)) // TILE
    mask = (lax.axis_index("frame") < valid[:, 0][:, None]) & (
        tile_ids[None, :] < valid[:, 1][:, None]
    )
    tokw = jnp.broadcast_to(mask.astype(jnp.float32)[:, :, None], (videos, span_dev, 128))
    shape = (videos, span_dev, width)
    mixed, total, _ = run_kernel(
        latents.reshape(shape), mod, tiles, frames_ok, tokw,
        w_sqkv, w_sout, w_tqkv, w_tout, target.reshape(shape),
    )
    count = jnp.sum(valid[:, 0] * valid[:, 1]).astype(jnp.float32) * TILE
    return (mixed.reshape(latents.shape), total[0, 0] / count)


def solution(mesh):
    return jax.shard_map(
        shards,
        mesh=mesh,
        in_specs=(
            P(None, "frame", "space", None),
            P(None, "frame", "space", None),
            P(),
            P(),
            P(),
            P(),
            P(None, None, "space"),
            P("space", None),
            P(None, None, "frame"),
            P("frame", None),
        ),
        out_specs=(P(None, "frame", "space", None), P()),
        check_vma=False,
    )
```

```python
import functools
import math

import jax
import jax.numpy as jnp
from jax import lax
from jax.experimental import pallas as pl
from jax.experimental.pallas import tpu as pltpu
from jax.sharding import PartitionSpec as P

HEAD_DIM = 128
FREQ = 256
TILE = 32
PAD = 128
MESH = pl.DeviceIdType.MESH


def time_embed(timesteps):
    half = FREQ // 2
    freqs = jnp.exp(-math.log(10000.0) * jnp.arange(half, dtype=jnp.float32) / half)
    angles = timesteps.astype(jnp.float32)[:, None] * freqs[None, :]
    return jnp.concatenate([jnp.cos(angles), jnp.sin(angles)], -1).astype(jnp.bfloat16)


def norm_mod(values, shift, scale):
    mean = jnp.mean(values, -1, keepdims=True)
    centred = values - mean
    var = jnp.mean(centred * centred, -1, keepdims=True)
    return (centred * lax.rsqrt(var + 1e-06) * (1.0 + scale) + shift).astype(jnp.bfloat16)


def attend(query, keys, values, allowed):
    scores = lax.dot_general(
        query, keys, (((1,), (1,)), ((), ())), preferred_element_type=jnp.float32
    ) * (1.0 / math.sqrt(HEAD_DIM))
    scores = jnp.where(allowed, scores, -1e30)
    top = jnp.max(scores, -1, keepdims=True)
    weights = jnp.exp(scores - top)
    probs = (weights * (1.0 / jnp.sum(weights, -1, keepdims=True))).astype(jnp.bfloat16)
    return jnp.dot(probs, values, preferred_element_type=jnp.float32).astype(jnp.bfloat16)


def expand(table, ids):
    rows = jnp.dot(ids, table, preferred_element_type=jnp.float32).astype(jnp.bfloat16)
    return lax.dot_general(rows, ids, (((1,), (1,)), ((), ())), preferred_element_type=jnp.float32)


def kernel(
    n_space, n_frame, offsets, nx, ny,
    lat_ref, mod_ref, tiles_ref, framesok_ref, tokw_ref, wq_hbm, wso_hbm, wt_hbm, wto_hbm, tgt_hbm,
    mixed_ref, loss_ref, W,
    G, PR, R, H, C, x1_ref, tgt, LS, LF, wq, wso, wt, qkv, att, tqkv, A, smask, tmask,
    ag_s, ag_r, fw_s, fw_r, pr_s, pr_r, rs_s, rs_r, z_s, z_r, a_s, a_r,
    wz_s, wz_r, wp_s, wp_r, ws_s, ws_r, l_s, l_r, lf_s, lf_r, w_sem, wl_sem,
):
    V, L, D = lat_ref.shape
    nch = n_space // 2
    span = n_space * L
    sp = lax.axis_index("space")
    fr = lax.axis_index("frame")
    core = sp % 2
    chip = sp // 2
    cx, cy = chip % nx, chip // nx
    no = len(offsets)

    def plus(k):
        dx, dy = offsets[k]
        return ((cy + dy) % ny) * nx + (cx + dx) % nx

    def minus(k):
        dx, dy = offsets[k]
        return ((cy + ny - dy) % ny) * nx + (cx + nx - dx) % nx

    FR = wto_hbm.shape[0]
    U = FR // n_space

    def unit(f, s):
        return W.at[pl.ds(pl.multiple_of(f * FR + s * U, U), U)]

    sib = {"space": chip * 2 + (1 - core)}

    loads = [
        pltpu.make_async_copy(wq_hbm, wq, w_sem.at[0]),
        pltpu.make_async_copy(wso_hbm, wso, w_sem.at[1]),
        pltpu.make_async_copy(wt_hbm, wt, w_sem.at[2]),
        pltpu.make_async_copy(tgt_hbm, tgt, w_sem.at[3]),
    ]
    for ld in loads:
        ld.start()

    bar = pltpu.get_barrier_semaphore()
    for o in range(1, n_space):
        pl.semaphore_signal(bar, inc=1, device_id={"space": (sp + o) % n_space}, device_id_type=MESH)
    for o in range(1, n_frame):
        pl.semaphore_signal(bar, inc=1, device_id={"frame": (fr + o) % n_frame}, device_id_type=MESH)

    def rcopy(src, dst, s, r, dev):
        return pltpu.make_async_remote_copy(
            src_ref=src, dst_ref=dst, send_sem=s, recv_sem=r, device_id=dev, device_id_type=MESH
        )

    def ag(v, k):
        return rcopy(
            G.at[v, chip, core], G.at[v, chip, core], ag_s.at[v, k], ag_r.at[v, k],
            {"space": plus(k) * 2 + core},
        )

    def ag_in(v, k):
        slot = G.at[v, minus(k), core]
        return rcopy(slot, slot, ag_s.at[v, k], ag_r.at[v, k], {"space": plus(k) * 2 + core})

    def fw(v, k):
        slot = G.at[v, minus(k), core]
        return rcopy(slot, slot, fw_s.at[v, k], fw_r.at[v, k], sib)

    def fw_in(v, k):
        slot = G.at[v, minus(k), 1 - core]
        return rcopy(slot, slot, fw_s.at[v, k], fw_r.at[v, k], sib)

    def pr(v, k):
        return rcopy(G.at[v, plus(k), 1 - core], PR.at[v, k], pr_s.at[v, k], pr_r.at[v, k], sib)

    def rs(v, k):
        return rcopy(
            G.at[v, plus(k), core], R.at[v, k], rs_s.at[v, k], rs_r.at[v, k],
            {"space": plus(k) * 2 + core},
        )

    def zg(v, o):
        return rcopy(
            H.at[v, fr], H.at[v, fr], z_s.at[v, o], z_r.at[v, o], {"frame": (fr + o) % n_frame}
        )

    def zg_in(v, o):
        slot = H.at[v, (fr + n_frame - o) % n_frame]
        return rcopy(slot, slot, z_s.at[v, o], z_r.at[v, o], {"frame": (fr + o) % n_frame})

    tc = tqkv.shape[2]

    def ax(v, o):
        cols = pl.ds(pl.multiple_of(fr * tc, tc), tc)
        dst = (fr + o) % n_frame
        return rcopy(
            A.at[v, dst], C.at[v, :, cols], a_s.at[v, o], a_r.at[v, o], {"frame": dst}
        )

    def ax_in(v, o):
        src = (fr + n_frame - o) % n_frame
        cols = pl.ds(pl.multiple_of(src * tc, tc), tc)
        return rcopy(
            A.at[v, src], C.at[v, :, cols], a_s.at[v, o], a_r.at[v, o], {"frame": src}
        )

    def wz(o):
        src = wto_hbm.at[pl.ds(pl.multiple_of(sp * U, U), U)]
        return rcopy(
            src, unit(fr, sp), wz_s.at[o], wz_r.at[o], {"frame": (fr + o) % n_frame}
        )

    def wz_in(o):
        slot = unit((fr + n_frame - o) % n_frame, sp)
        return rcopy(slot, slot, wz_s.at[o], wz_r.at[o], {"frame": (fr + o) % n_frame})

    def wp(o, k):
        slot = unit((fr + n_frame - o) % n_frame, sp)
        return rcopy(slot, slot, wp_s.at[o, k], wp_r.at[o, k], {"space": plus(k) * 2 + core})

    def wp_in(o, k):
        slot = unit((fr + n_frame - o) % n_frame, minus(k) * 2 + core)
        return rcopy(slot, slot, wp_s.at[o, k], wp_r.at[o, k], {"space": plus(k) * 2 + core})

    def ws(o, k):
        slot = unit((fr + n_frame - o) % n_frame, minus(k) * 2 + core)
        return rcopy(slot, slot, ws_s.at[o, k], ws_r.at[o, k], sib)

    def ws_in(o, k):
        slot = unit((fr + n_frame - o) % n_frame, minus(k) * 2 + 1 - core)
        return rcopy(slot, slot, ws_s.at[o, k], ws_r.at[o, k], sib)

    def ls(o):
        return rcopy(
            LS.at[sp], LS.at[sp], l_s.at[o], l_r.at[o], {"space": (sp + o) % n_space}
        )

    def ls_in(o):
        slot = LS.at[(sp + n_space - o) % n_space]
        return rcopy(slot, slot, l_s.at[o], l_r.at[o], {"space": (sp + o) % n_space})

    def lf(o):
        return rcopy(
            LF.at[fr], LF.at[fr], lf_s.at[o], lf_r.at[o], {"frame": (fr + o) % n_frame}
        )

    def lf_in(o):
        slot = LF.at[(fr + n_frame - o) % n_frame]
        return rcopy(slot, slot, lf_s.at[o], lf_r.at[o], {"frame": (fr + o) % n_frame})

    def mod(v, i):
        return mod_ref[v, i : i + 1, :]

    for v in range(V):
        G[v, chip, core] = norm_mod(lat_ref[v].astype(jnp.float32), mod(v, 0), mod(v, 1))
        if v == 0:
            pl.semaphore_wait(bar, (n_space - 1) + (n_frame - 1))
        for k in range(no - 1, 0, -1):
            ag(v, k).start()
        fw(v, 0).start()
    for o in range(1, n_frame):
        wz(o).start()

    row = lax.broadcasted_iota(jnp.int32, (span, PAD), 0) // TILE
    col = lax.broadcasted_iota(jnp.int32, (span, PAD), 1)
    tile_ids = (row == col).astype(jnp.bfloat16)
    tl = n_frame * L
    rowf = lax.broadcasted_iota(jnp.int32, (tl, PAD), 0) // L
    colf = lax.broadcasted_iota(jnp.int32, (tl, PAD), 1)
    frame_ids = (rowf == colf).astype(jnp.bfloat16)
    place_q = lax.broadcasted_iota(jnp.int32, (tl, tl), 0) % L
    place_k = lax.broadcasted_iota(jnp.int32, (tl, tl), 1) % L
    for v in range(V):
        smask[v] = expand(tiles_ref[v], tile_ids).astype(jnp.bfloat16)
        both = jnp.where(place_q == place_k, expand(framesok_ref[v], frame_ids), 0.0)
        tmask[v] = both.astype(jnp.bfloat16)

    def forward(v):
        for k in range(1, no):
            ag_in(v, k).wait_recv()
            fw(v, k).start()

    sc = qkv.shape[2]
    QB = 256

    def spatial(v):
        for k in range(no):
            fw_in(v, k).wait_recv()
        if v == 0:
            loads[0].wait()
        mt = 256 // (2 * L)
        nm = nch // mt

        def qkv_step(i, _):
            j, m = i // nm, i % nm
            x = G[v, pl.ds(m * mt, mt)].reshape(256, D)
            qkv[j, pl.ds(pl.multiple_of(m * 256, 256), 256), :] = jnp.dot(
                x, wq[j], preferred_element_type=jnp.float32
            ).astype(jnp.bfloat16)
            return 0

        lax.fori_loop(0, 3 * nm, qkv_step, 0)

        for h in range(sc // HEAD_DIM):
            hs = slice(h * HEAD_DIM, (h + 1) * HEAD_DIM)

            def att_step(i, _):
                rows = pl.ds(pl.multiple_of(i * QB, QB), QB)
                ok = smask[v, rows, :].astype(jnp.float32) > 0.5
                att[rows, hs] = attend(qkv[0, rows, hs], qkv[1, :, hs], qkv[2, :, hs], ok)
                return 0

            lax.fori_loop(0, span // QB, att_step, 0)

        for k in range(1, no):
            ag(v, k).wait_send()
        for k in range(no):
            fw(v, k).wait_send()
        if v == 0:
            loads[1].wait()

        CB = 512

        def term_step(i, _):
            cols = pl.ds(pl.multiple_of(i * CB, CB), CB)
            t = jnp.dot(att[...], wso[:, cols], preferred_element_type=jnp.float32)
            G[v, :, :, :, cols] = t.astype(jnp.bfloat16).reshape(nch, 2, L, CB)
            return 0

        lax.fori_loop(0, D // CB, term_step, 0)
        for k in range(no - 1, -1, -1):
            pr(v, k).start()

    def reduce_send(v):
        for k in range(no - 1, 0, -1):
            pr(v, k).wait_recv()
            c = plus(k)
            G[v, c, core] = (
                G[v, c, core].astype(jnp.float32) + PR[v, k].astype(jnp.float32)
            ).astype(jnp.bfloat16)
            rs(v, k).start()

    def finish_spatial(v):
        pr(v, 0).wait_recv()
        so = G[v, chip, core].astype(jnp.float32) + PR[v, 0].astype(jnp.float32)
        for k in range(1, no):
            rs(v, k).wait_recv()
            so = so + R[v, k].astype(jnp.float32)
        x1 = (lat_ref[v].astype(jnp.float32) + mod(v, 2) * so).astype(jnp.bfloat16)
        x1_ref[v] = x1
        H[v, fr] = norm_mod(x1.astype(jnp.float32), mod(v, 3), mod(v, 4))
        for o in range(1, n_frame):
            zg(v, o).start()

    def temporal(v):
        for o in range(1, n_frame):
            zg_in(v, o).wait_recv()
        if v == 0:
            loads[2].wait()
        NB = 256
        nn = tc // NB

        def tqkv_step(i, _):
            j, n = i // nn, i % nn
            cols = pl.ds(pl.multiple_of(n * NB, NB), NB)
            tqkv[j, :, cols] = jnp.dot(
                H[v].reshape(tl, D), wt[j, :, cols], preferred_element_type=jnp.float32
            ).astype(jnp.bfloat16)
            return 0

        lax.fori_loop(0, 3 * nn, tqkv_step, 0)
        ok = tmask[v].astype(jnp.float32) > 0.5
        for h in range(tc // HEAD_DIM):
            hs = slice(h * HEAD_DIM, (h + 1) * HEAD_DIM)
            out = attend(tqkv[0, :, hs], tqkv[1, :, hs], tqkv[2, :, hs], ok)
            A[v, :, :, hs] = out.reshape(n_frame, L, HEAD_DIM)
        for o in range(1, n_frame):
            ax(v, o).start()
        C[v, :, pl.ds(pl.multiple_of(fr * tc, tc), tc)] = A[v, fr]

    forward(0)
    spatial(0)
    reduce_send(0)
    forward(1)
    spatial(1)
    reduce_send(1)
    finish_spatial(0)
    finish_spatial(1)
    for o in range(1, n_frame):
        wz_in(o).wait_recv()
        for k in range(no - 1, 0, -1):
            wp(o, k).start()
        ws(o, 0).start()
    temporal(0)
    for o in range(1, n_frame):
        for k in range(1, no):
            wp_in(o, k).wait_recv()
            ws(o, k).start()
    temporal(1)

    for v in range(V):
        for k in range(no):
            pr(v, k).wait_send()
        for k in range(1, no):
            rs(v, k).wait_send()
    for o in range(1, n_frame):
        for k in range(no):
            ws_in(o, k).wait_recv()
    rows = FR * n_frame
    slots = [G.at[v, c, e] for v in range(V) for c in range(nch) for e in range(2)]
    slots += [PR.at[v, k] for v in range(V) for k in range(no)]
    slots += [R.at[v, k] for v in range(V) for k in range(no)]

    def from_frame(row):
        start = ((fr + n_frame - row // FR) % n_frame) * FR + row % FR
        return pl.multiple_of(start, L)

    pulls = [
        pltpu.make_async_copy(
            wto_hbm.at[pl.ds(b * L, L)] if b * L < FR else W.at[pl.ds(from_frame(b * L), L)],
            slots[b],
            wl_sem.at[b],
        )
        for b in range(rows // L)
    ]
    for p in pulls:
        p.start()
    quads = [(G, v, c) for v in range(V) for c in range(0, nch, 2)]
    quads += [(PR, v, k) for v in range(V) for k in range(0, no, 4)]
    quads += [(R, v, k) for v in range(V) for k in range(0, no, 4)]
    quads = quads[: rows // (4 * L)]
    for v in range(V):
        for o in range(1, n_frame):
            ax_in(v, o).wait_recv()
    loads[3].wait()
    for p in pulls:
        p.wait()
    CB = 512

    def out_step(i, total):
        cols = pl.ds(pl.multiple_of(i * CB, CB), CB)
        acc = jnp.zeros((V * L, CB), jnp.float32)
        for q, (buf, v, c) in enumerate(quads):
            if buf is G:
                w = buf[v, c : c + 2, :, :, cols].reshape(4 * L, CB)
            else:
                w = buf[v, c : c + 4, :, cols].reshape(4 * L, CB)
            mine = pl.ds(pl.multiple_of(from_frame(q * 4 * L), 4 * L), 4 * L)
            a = C[:, :, mine].reshape(V * L, 4 * L)
            acc = acc + jnp.dot(a, w, preferred_element_type=jnp.float32)
        part = []
        for v in range(V):
            gate = mod_ref[v, 5:6, cols]
            m = x1_ref[v, :, cols].astype(jnp.float32) + gate * acc[v * L : (v + 1) * L]
            m = m.astype(jnp.bfloat16)
            mixed_ref[v, :, cols] = m
            diff = m.astype(jnp.float32) - tgt[v, :, cols].astype(jnp.float32)
            part.append(jnp.sum(diff * diff, -1, keepdims=True))
        return total + jnp.concatenate(part, 0)

    squares = lax.fori_loop(0, D // CB, out_step, jnp.zeros((V * L, 1), jnp.float32)) * (1.0 / D)
    kept = squares.reshape(V, L, 1) * tokw_ref[...]
    LS[sp] = jnp.broadcast_to(jnp.sum(jnp.sum(kept, 0), 0, keepdims=True), (8, 128))
    for o in range(1, n_space):
        ls(o).start()
    for o in range(1, n_space):
        ls_in(o).wait_recv()
    LF[fr] = jnp.sum(LS[...], 0)
    for o in range(1, n_frame):
        lf(o).start()
    for o in range(1, n_frame):
        lf_in(o).wait_recv()
    loss_ref[...] = jnp.sum(LF[...], 0)

    for v in range(V):
        for o in range(1, n_frame):
            zg(v, o).wait_send()
            ax(v, o).wait_send()
    for o in range(1, n_frame):
        wz(o).wait_send()
        lf(o).wait_send()
        for k in range(no):
            ws(o, k).wait_send()
        for k in range(1, no):
            wp(o, k).wait_send()
    for o in range(1, n_space):
        ls(o).wait_send()


def run_kernel(latents, mod, tiles, frames_ok, tokw, w_sqkv, w_sout, w_tqkv, w_tout, target):
    V, L, D = latents.shape
    n_space = lax.axis_size("space")
    n_frame = lax.axis_size("frame")
    nch = n_space // 2
    ny = 2 if nch % 2 == 0 else 1
    nx = nch // ny
    offsets = [(dx, dy) for dy in range(ny) for dx in range(nx)]
    no = len(offsets)
    sc, tc = w_sqkv.shape[2], w_tqkv.shape[2]
    span = n_space * L
    tl = n_frame * L
    bf = jnp.bfloat16
    dma = pltpu.SemaphoreType.DMA
    vm = pl.BlockSpec(memory_space=pltpu.VMEM)
    hbm = pl.BlockSpec(memory_space=pl.ANY)
    return pl.pallas_call(
        functools.partial(kernel, n_space, n_frame, offsets, nx, ny),
        out_shape=(
            jax.ShapeDtypeStruct((V, L, D), bf),
            jax.ShapeDtypeStruct((8, 128), jnp.float32),
            jax.ShapeDtypeStruct((n_frame * w_tout.shape[0], D), bf),
        ),
        in_specs=[vm, vm, vm, vm, vm, hbm, hbm, hbm, hbm, hbm],
        out_specs=(vm, vm, hbm),
        scratch_shapes=[
            pltpu.VMEM((V, nch, 2, L, D), bf),
            pltpu.VMEM((V, no, L, D), bf),
            pltpu.VMEM((V, no, L, D), bf),
            pltpu.VMEM((V, n_frame, L, D), bf),
            pltpu.VMEM((V, L, n_frame * tc), bf),
            pltpu.VMEM((V, L, D), bf),
            pltpu.VMEM((V, L, D), bf),
            pltpu.VMEM((n_space, 8, 128), jnp.float32),
            pltpu.VMEM((n_frame, 8, 128), jnp.float32),
            pltpu.VMEM(w_sqkv.shape, bf),
            pltpu.VMEM(w_sout.shape, bf),
            pltpu.VMEM(w_tqkv.shape, bf),
            pltpu.VMEM((3, span, sc), bf),
            pltpu.VMEM((span, sc), bf),
            pltpu.VMEM((3, tl, tc), bf),
            pltpu.VMEM((V, n_frame, L, tc), bf),
            pltpu.VMEM((V, span, span), bf),
            pltpu.VMEM((V, tl, tl), bf),
            dma((V, no)), dma((V, no)), dma((V, no)), dma((V, no)),
            dma((V, no)), dma((V, no)), dma((V, no)), dma((V, no)),
            dma((V, n_frame)), dma((V, n_frame)), dma((V, n_frame)), dma((V, n_frame)),
            dma((n_frame,)), dma((n_frame,)), dma((n_frame, no)), dma((n_frame, no)),
            dma((n_frame, no)), dma((n_frame, no)), dma((n_space,)), dma((n_space,)),
            dma((n_frame,)), dma((n_frame,)), dma((4,)), dma((n_frame * w_tout.shape[0] // L,)),
        ],
        compiler_params=pltpu.CompilerParams(
            collective_id=0, has_side_effects=True, vmem_limit_bytes=60 * 1024 * 1024
        ),
        cost_estimate=pl.CostEstimate(
            flops=20_000_000_000, bytes_accessed=300_000_000, transcendentals=3_000_000
        ),
        name="block",
    )(latents, mod, tiles, frames_ok, tokw, w_sqkv, w_sout, w_tqkv, w_tout, target)


def shards(latents, target, timesteps, valid, tile_mask, w_mod, w_sqkv, w_sout, w_tqkv, w_tout):
    videos, frames_dev, span_dev, width = latents.shape
    embed = time_embed(timesteps)
    mod = jnp.dot(embed, w_mod, preferred_element_type=jnp.float32).reshape(videos, 6, width)
    nt = tile_mask.shape[1]
    t_ids = jnp.arange(nt, dtype=jnp.int32)
    tiles = ((tile_mask == 1) & (t_ids[None, None, :] < valid[:, 1][:, None, None])) | (
        t_ids[None, :, None] == t_ids[None, None, :]
    )
    tiles = jnp.pad(tiles.astype(jnp.bfloat16), ((0, 0), (0, PAD - nt), (0, PAD - nt)))
    p_ids = jnp.arange(PAD, dtype=jnp.int32)
    frames_ok = (
        (p_ids[None, None, :] < valid[:, 0][:, None, None])
        | (p_ids[None, :, None] == p_ids[None, None, :])
    ).astype(jnp.bfloat16)
    tile_ids = (lax.axis_index("space") * span_dev + jnp.arange(span_dev, dtype=jnp.int32)) // TILE
    mask = (lax.axis_index("frame") < valid[:, 0][:, None]) & (
        tile_ids[None, :] < valid[:, 1][:, None]
    )
    tokw = jnp.broadcast_to(mask.astype(jnp.float32)[:, :, None], (videos, span_dev, 128))
    shape = (videos, span_dev, width)
    mixed, total, _ = run_kernel(
        latents.reshape(shape), mod, tiles, frames_ok, tokw,
        w_sqkv, w_sout, w_tqkv, w_tout, target.reshape(shape),
    )
    count = jnp.sum(valid[:, 0] * valid[:, 1]).astype(jnp.float32) * TILE
    return (mixed.reshape(latents.shape), total[0, 0] / count)


def solution(mesh):
    return jax.shard_map(
        shards,
        mesh=mesh,
        in_specs=(
            P(None, "frame", "space", None),
            P(None, "frame", "space", None),
            P(),
            P(),
            P(),
            P(),
            P(None, None, "space"),
            P("space", None),
            P(None, None, "frame"),
            P("frame", None),
        ),
        out_specs=(P(None, "frame", "space", None), P()),
        check_vma=False,
    )
```

```python
import functools
import math

import jax
import jax.numpy as jnp
from jax import lax
from jax.experimental import pallas as pl
from jax.experimental.pallas import tpu as pltpu
from jax.sharding import PartitionSpec as P

HEAD_DIM = 128
FREQ = 256
TILE = 32
PAD = 128
MESH = pl.DeviceIdType.MESH


def time_embed(timesteps):
    half = FREQ // 2
    freqs = jnp.exp(-math.log(10000.0) * jnp.arange(half, dtype=jnp.float32) / half)
    angles = timesteps.astype(jnp.float32)[:, None] * freqs[None, :]
    return jnp.concatenate([jnp.cos(angles), jnp.sin(angles)], -1).astype(jnp.bfloat16)


def norm_mod(values, shift, scale):
    mean = jnp.mean(values, -1, keepdims=True)
    centred = values - mean
    var = jnp.mean(centred * centred, -1, keepdims=True)
    return (centred * lax.rsqrt(var + 1e-06) * (1.0 + scale) + shift).astype(jnp.bfloat16)


def attend(query, keys, values, allowed):
    scores = lax.dot_general(
        query, keys, (((1,), (1,)), ((), ())), preferred_element_type=jnp.float32
    ) * (1.0 / math.sqrt(HEAD_DIM))
    scores = jnp.where(allowed, scores, -1e30)
    top = jnp.max(scores, -1, keepdims=True)
    weights = jnp.exp(scores - top)
    probs = (weights * (1.0 / jnp.sum(weights, -1, keepdims=True))).astype(jnp.bfloat16)
    return jnp.dot(probs, values, preferred_element_type=jnp.float32).astype(jnp.bfloat16)


def expand(table, ids):
    rows = jnp.dot(ids, table, preferred_element_type=jnp.float32).astype(jnp.bfloat16)
    return lax.dot_general(rows, ids, (((1,), (1,)), ((), ())), preferred_element_type=jnp.float32)


def kernel(
    n_space, n_frame, offsets, nx, ny,
    lat_ref, mod_ref, tiles_ref, framesok_ref, tokw_ref, wq_hbm, wso_hbm, wt_hbm, wto_hbm, tgt_hbm,
    mixed_ref, loss_ref, W,
    G, PR, R, H, C, x1_ref, tgt, LS, LF, wq, wso, wt, qkv, att, tqkv, A, smask, tmask,
    ag_s, ag_r, fw_s, fw_r, pr_s, pr_r, rs_s, rs_r, z_s, z_r, a_s, a_r,
    wz_s, wz_r, wp_s, wp_r, ws_s, ws_r, l_s, l_r, lf_s, lf_r, w_sem, wl_sem,
):
    V, L, D = lat_ref.shape
    nch = n_space // 2
    span = n_space * L
    sp = lax.axis_index("space")
    fr = lax.axis_index("frame")
    core = sp % 2
    chip = sp // 2
    cx, cy = chip % nx, chip // nx
    no = len(offsets)

    def plus(k):
        dx, dy = offsets[k]
        return ((cy + dy) % ny) * nx + (cx + dx) % nx

    def minus(k):
        dx, dy = offsets[k]
        return ((cy + ny - dy) % ny) * nx + (cx + nx - dx) % nx

    FR = wto_hbm.shape[0]
    U = FR // n_space

    def unit(f, s):
        return W.at[pl.ds(pl.multiple_of(f * FR + s * U, U), U)]

    sib = {"space": chip * 2 + (1 - core)}

    loads = [
        pltpu.make_async_copy(wq_hbm, wq, w_sem.at[0]),
        pltpu.make_async_copy(wso_hbm, wso, w_sem.at[1]),
        pltpu.make_async_copy(wt_hbm, wt, w_sem.at[2]),
        pltpu.make_async_copy(tgt_hbm, tgt, w_sem.at[3]),
    ]
    for ld in loads:
        ld.start()

    bar = pltpu.get_barrier_semaphore()
    for o in range(1, n_space):
        pl.semaphore_signal(bar, inc=1, device_id={"space": (sp + o) % n_space}, device_id_type=MESH)
    for o in range(1, n_frame):
        pl.semaphore_signal(bar, inc=1, device_id={"frame": (fr + o) % n_frame}, device_id_type=MESH)

    def rcopy(src, dst, s, r, dev):
        return pltpu.make_async_remote_copy(
            src_ref=src, dst_ref=dst, send_sem=s, recv_sem=r, device_id=dev, device_id_type=MESH
        )

    def ag(v, k):
        return rcopy(
            G.at[v, chip, core], G.at[v, chip, core], ag_s.at[v, k], ag_r.at[v, k],
            {"space": plus(k) * 2 + core},
        )

    def ag_in(v, k):
        slot = G.at[v, minus(k), core]
        return rcopy(slot, slot, ag_s.at[v, k], ag_r.at[v, k], {"space": plus(k) * 2 + core})

    def fw(v, k):
        slot = G.at[v, minus(k), core]
        return rcopy(slot, slot, fw_s.at[v, k], fw_r.at[v, k], sib)

    def fw_in(v, k):
        slot = G.at[v, minus(k), 1 - core]
        return rcopy(slot, slot, fw_s.at[v, k], fw_r.at[v, k], sib)

    def pr(v, k):
        return rcopy(G.at[v, plus(k), 1 - core], PR.at[v, k], pr_s.at[v, k], pr_r.at[v, k], sib)

    def rs(v, k):
        return rcopy(
            G.at[v, plus(k), core], R.at[v, k], rs_s.at[v, k], rs_r.at[v, k],
            {"space": plus(k) * 2 + core},
        )

    def zg(v, o):
        return rcopy(
            H.at[v, fr], H.at[v, fr], z_s.at[v, o], z_r.at[v, o], {"frame": (fr + o) % n_frame}
        )

    def zg_in(v, o):
        slot = H.at[v, (fr + n_frame - o) % n_frame]
        return rcopy(slot, slot, z_s.at[v, o], z_r.at[v, o], {"frame": (fr + o) % n_frame})

    tc = tqkv.shape[2]

    def ax(v, o):
        cols = pl.ds(pl.multiple_of(fr * tc, tc), tc)
        dst = (fr + o) % n_frame
        return rcopy(
            A.at[v, dst], C.at[v, :, cols], a_s.at[v, o], a_r.at[v, o], {"frame": dst}
        )

    def ax_in(v, o):
        src = (fr + n_frame - o) % n_frame
        cols = pl.ds(pl.multiple_of(src * tc, tc), tc)
        return rcopy(
            A.at[v, src], C.at[v, :, cols], a_s.at[v, o], a_r.at[v, o], {"frame": src}
        )

    def wz(o):
        src = wto_hbm.at[pl.ds(pl.multiple_of(sp * U, U), U)]
        return rcopy(
            src, unit(fr, sp), wz_s.at[o], wz_r.at[o], {"frame": (fr + o) % n_frame}
        )

    def wz_in(o):
        slot = unit((fr + n_frame - o) % n_frame, sp)
        return rcopy(slot, slot, wz_s.at[o], wz_r.at[o], {"frame": (fr + o) % n_frame})

    def wp(o, k):
        slot = unit((fr + n_frame - o) % n_frame, sp)
        return rcopy(slot, slot, wp_s.at[o, k], wp_r.at[o, k], {"space": plus(k) * 2 + core})

    def wp_in(o, k):
        slot = unit((fr + n_frame - o) % n_frame, minus(k) * 2 + core)
        return rcopy(slot, slot, wp_s.at[o, k], wp_r.at[o, k], {"space": plus(k) * 2 + core})

    def ws(o, k):
        slot = unit((fr + n_frame - o) % n_frame, minus(k) * 2 + core)
        return rcopy(slot, slot, ws_s.at[o, k], ws_r.at[o, k], sib)

    def ws_in(o, k):
        slot = unit((fr + n_frame - o) % n_frame, minus(k) * 2 + 1 - core)
        return rcopy(slot, slot, ws_s.at[o, k], ws_r.at[o, k], sib)

    def ls(o):
        return rcopy(
            LS.at[sp], LS.at[sp], l_s.at[o], l_r.at[o], {"space": (sp + o) % n_space}
        )

    def ls_in(o):
        slot = LS.at[(sp + n_space - o) % n_space]
        return rcopy(slot, slot, l_s.at[o], l_r.at[o], {"space": (sp + o) % n_space})

    def lf(o):
        return rcopy(
            LF.at[fr], LF.at[fr], lf_s.at[o], lf_r.at[o], {"frame": (fr + o) % n_frame}
        )

    def lf_in(o):
        slot = LF.at[(fr + n_frame - o) % n_frame]
        return rcopy(slot, slot, lf_s.at[o], lf_r.at[o], {"frame": (fr + o) % n_frame})

    def mod(v, i):
        return mod_ref[v, i : i + 1, :]

    for v in range(V):
        G[v, chip, core] = norm_mod(lat_ref[v].astype(jnp.float32), mod(v, 0), mod(v, 1))
        if v == 0:
            pl.semaphore_wait(bar, (n_space - 1) + (n_frame - 1))
        for k in range(no - 1, 0, -1):
            ag(v, k).start()
        fw(v, 0).start()
    for o in range(1, n_frame):
        wz(o).start()

    row = lax.broadcasted_iota(jnp.int32, (span, PAD), 0) // TILE
    col = lax.broadcasted_iota(jnp.int32, (span, PAD), 1)
    tile_ids = (row == col).astype(jnp.bfloat16)
    tl = n_frame * L
    rowf = lax.broadcasted_iota(jnp.int32, (tl, PAD), 0) // L
    colf = lax.broadcasted_iota(jnp.int32, (tl, PAD), 1)
    frame_ids = (rowf == colf).astype(jnp.bfloat16)
    place_q = lax.broadcasted_iota(jnp.int32, (tl, tl), 0) % L
    place_k = lax.broadcasted_iota(jnp.int32, (tl, tl), 1) % L
    for v in range(V):
        smask[v] = expand(tiles_ref[v], tile_ids).astype(jnp.bfloat16)
        both = jnp.where(place_q == place_k, expand(framesok_ref[v], frame_ids), 0.0)
        tmask[v] = both.astype(jnp.bfloat16)

    def forward(v):
        for k in range(1, no):
            ag_in(v, k).wait_recv()
            fw(v, k).start()

    sc = qkv.shape[2]
    QB = 256

    def spatial(v):
        for k in range(no):
            fw_in(v, k).wait_recv()
        if v == 0:
            loads[0].wait()
        mt = 256 // (2 * L)
        nm = nch // mt

        def qkv_step(i, _):
            j, m = i // nm, i % nm
            x = G[v, pl.ds(m * mt, mt)].reshape(256, D)
            qkv[j, pl.ds(pl.multiple_of(m * 256, 256), 256), :] = jnp.dot(
                x, wq[j], preferred_element_type=jnp.float32
            ).astype(jnp.bfloat16)
            return 0

        lax.fori_loop(0, 3 * nm, qkv_step, 0)

        for h in range(sc // HEAD_DIM):
            hs = slice(h * HEAD_DIM, (h + 1) * HEAD_DIM)

            def att_step(i, _):
                rows = pl.ds(pl.multiple_of(i * QB, QB), QB)
                ok = smask[v, rows, :].astype(jnp.float32) > 0.5
                att[rows, hs] = attend(qkv[0, rows, hs], qkv[1, :, hs], qkv[2, :, hs], ok)
                return 0

            lax.fori_loop(0, span // QB, att_step, 0)

        for k in range(1, no):
            ag(v, k).wait_send()
        for k in range(no):
            fw(v, k).wait_send()
        if v == 0:
            loads[1].wait()

        CB = 512

        def term_step(i, _):
            cols = pl.ds(pl.multiple_of(i * CB, CB), CB)
            t = jnp.dot(att[...], wso[:, cols], preferred_element_type=jnp.float32)
            G[v, :, :, :, cols] = t.astype(jnp.bfloat16).reshape(nch, 2, L, CB)
            return 0

        lax.fori_loop(0, D // CB, term_step, 0)
        for k in range(no - 1, -1, -1):
            pr(v, k).start()

    def reduce_send(v):
        for k in range(no - 1, 0, -1):
            pr(v, k).wait_recv()
            c = plus(k)
            G[v, c, core] = (
                G[v, c, core].astype(jnp.float32) + PR[v, k].astype(jnp.float32)
            ).astype(jnp.bfloat16)
            rs(v, k).start()

    def finish_spatial(v):
        pr(v, 0).wait_recv()
        so = G[v, chip, core].astype(jnp.float32) + PR[v, 0].astype(jnp.float32)
        for k in range(1, no):
            rs(v, k).wait_recv()
            so = so + R[v, k].astype(jnp.float32)
        x1 = (lat_ref[v].astype(jnp.float32) + mod(v, 2) * so).astype(jnp.bfloat16)
        x1_ref[v] = x1
        H[v, fr] = norm_mod(x1.astype(jnp.float32), mod(v, 3), mod(v, 4))
        for o in range(1, n_frame):
            zg(v, o).start()

    def temporal(v):
        for o in range(1, n_frame):
            zg_in(v, o).wait_recv()
        if v == 0:
            loads[2].wait()
        NB = 256
        nn = tc // NB

        def tqkv_step(i, _):
            j, n = i // nn, i % nn
            cols = pl.ds(pl.multiple_of(n * NB, NB), NB)
            tqkv[j, :, cols] = jnp.dot(
                H[v].reshape(tl, D), wt[j, :, cols], preferred_element_type=jnp.float32
            ).astype(jnp.bfloat16)
            return 0

        lax.fori_loop(0, 3 * nn, tqkv_step, 0)
        ok = tmask[v].astype(jnp.float32) > 0.5
        for h in range(tc // HEAD_DIM):
            hs = slice(h * HEAD_DIM, (h + 1) * HEAD_DIM)
            out = attend(tqkv[0, :, hs], tqkv[1, :, hs], tqkv[2, :, hs], ok)
            A[v, :, :, hs] = out.reshape(n_frame, L, HEAD_DIM)
        for o in range(1, n_frame):
            ax(v, o).start()
        C[v, :, pl.ds(pl.multiple_of(fr * tc, tc), tc)] = A[v, fr]

    forward(0)
    spatial(0)
    reduce_send(0)
    forward(1)
    finish_spatial(0)
    spatial(1)
    reduce_send(1)
    finish_spatial(1)
    for o in range(1, n_frame):
        wz_in(o).wait_recv()
        for k in range(no - 1, 0, -1):
            wp(o, k).start()
        ws(o, 0).start()
    temporal(0)
    for o in range(1, n_frame):
        for k in range(1, no):
            wp_in(o, k).wait_recv()
            ws(o, k).start()
    temporal(1)

    for v in range(V):
        for k in range(no):
            pr(v, k).wait_send()
        for k in range(1, no):
            rs(v, k).wait_send()
    for o in range(1, n_frame):
        for k in range(no):
            ws_in(o, k).wait_recv()
    rows = FR * n_frame
    slots = [G.at[v, c, e] for v in range(V) for c in range(nch) for e in range(2)]
    slots += [PR.at[v, k] for v in range(V) for k in range(no)]
    slots += [R.at[v, k] for v in range(V) for k in range(no)]

    def from_frame(row):
        start = ((fr + n_frame - row // FR) % n_frame) * FR + row % FR
        return pl.multiple_of(start, L)

    pulls = [
        pltpu.make_async_copy(
            wto_hbm.at[pl.ds(b * L, L)] if b * L < FR else W.at[pl.ds(from_frame(b * L), L)],
            slots[b],
            wl_sem.at[b],
        )
        for b in range(rows // L)
    ]
    for p in pulls:
        p.start()
    quads = [(G, v, c) for v in range(V) for c in range(0, nch, 2)]
    quads += [(PR, v, k) for v in range(V) for k in range(0, no, 4)]
    quads += [(R, v, k) for v in range(V) for k in range(0, no, 4)]
    quads = quads[: rows // (4 * L)]
    for v in range(V):
        for o in range(1, n_frame):
            ax_in(v, o).wait_recv()
    loads[3].wait()
    for p in pulls:
        p.wait()
    CB = 512

    def out_step(i, total):
        cols = pl.ds(pl.multiple_of(i * CB, CB), CB)
        acc = jnp.zeros((V * L, CB), jnp.float32)
        for q, (buf, v, c) in enumerate(quads):
            if buf is G:
                w = buf[v, c : c + 2, :, :, cols].reshape(4 * L, CB)
            else:
                w = buf[v, c : c + 4, :, cols].reshape(4 * L, CB)
            mine = pl.ds(pl.multiple_of(from_frame(q * 4 * L), 4 * L), 4 * L)
            a = C[:, :, mine].reshape(V * L, 4 * L)
            acc = acc + jnp.dot(a, w, preferred_element_type=jnp.float32)
        part = []
        for v in range(V):
            gate = mod_ref[v, 5:6, cols]
            m = x1_ref[v, :, cols].astype(jnp.float32) + gate * acc[v * L : (v + 1) * L]
            m = m.astype(jnp.bfloat16)
            mixed_ref[v, :, cols] = m
            diff = m.astype(jnp.float32) - tgt[v, :, cols].astype(jnp.float32)
            part.append(jnp.sum(diff * diff, -1, keepdims=True))
        return total + jnp.concatenate(part, 0)

    squares = lax.fori_loop(0, D // CB, out_step, jnp.zeros((V * L, 1), jnp.float32)) * (1.0 / D)
    kept = squares.reshape(V, L, 1) * tokw_ref[...]
    LS[sp] = jnp.broadcast_to(jnp.sum(jnp.sum(kept, 0), 0, keepdims=True), (8, 128))
    for o in range(1, n_space):
        ls(o).start()
    for o in range(1, n_space):
        ls_in(o).wait_recv()
    LF[fr] = jnp.sum(LS[...], 0)
    for o in range(1, n_frame):
        lf(o).start()
    for o in range(1, n_frame):
        lf_in(o).wait_recv()
    loss_ref[...] = jnp.sum(LF[...], 0)

    for v in range(V):
        for o in range(1, n_frame):
            zg(v, o).wait_send()
            ax(v, o).wait_send()
    for o in range(1, n_frame):
        wz(o).wait_send()
        lf(o).wait_send()
        for k in range(no):
            ws(o, k).wait_send()
        for k in range(1, no):
            wp(o, k).wait_send()
    for o in range(1, n_space):
        ls(o).wait_send()


def run_kernel(latents, mod, tiles, frames_ok, tokw, w_sqkv, w_sout, w_tqkv, w_tout, target):
    V, L, D = latents.shape
    n_space = lax.axis_size("space")
    n_frame = lax.axis_size("frame")
    nch = n_space // 2
    ny = 2 if nch % 2 == 0 else 1
    nx = nch // ny
    offsets = [(dx, dy) for dy in range(ny) for dx in range(nx)]
    no = len(offsets)
    sc, tc = w_sqkv.shape[2], w_tqkv.shape[2]
    span = n_space * L
    tl = n_frame * L
    bf = jnp.bfloat16
    dma = pltpu.SemaphoreType.DMA
    vm = pl.BlockSpec(memory_space=pltpu.VMEM)
    hbm = pl.BlockSpec(memory_space=pl.ANY)
    return pl.pallas_call(
        functools.partial(kernel, n_space, n_frame, offsets, nx, ny),
        out_shape=(
            jax.ShapeDtypeStruct((V, L, D), bf),
            jax.ShapeDtypeStruct((8, 128), jnp.float32),
            jax.ShapeDtypeStruct((n_frame * w_tout.shape[0], D), bf),
        ),
        in_specs=[vm, vm, vm, vm, vm, hbm, hbm, hbm, hbm, hbm],
        out_specs=(vm, vm, hbm),
        scratch_shapes=[
            pltpu.VMEM((V, nch, 2, L, D), bf),
            pltpu.VMEM((V, no, L, D), bf),
            pltpu.VMEM((V, no, L, D), bf),
            pltpu.VMEM((V, n_frame, L, D), bf),
            pltpu.VMEM((V, L, n_frame * tc), bf),
            pltpu.VMEM((V, L, D), bf),
            pltpu.VMEM((V, L, D), bf),
            pltpu.VMEM((n_space, 8, 128), jnp.float32),
            pltpu.VMEM((n_frame, 8, 128), jnp.float32),
            pltpu.VMEM(w_sqkv.shape, bf),
            pltpu.VMEM(w_sout.shape, bf),
            pltpu.VMEM(w_tqkv.shape, bf),
            pltpu.VMEM((3, span, sc), bf),
            pltpu.VMEM((span, sc), bf),
            pltpu.VMEM((3, tl, tc), bf),
            pltpu.VMEM((V, n_frame, L, tc), bf),
            pltpu.VMEM((V, span, span), bf),
            pltpu.VMEM((V, tl, tl), bf),
            dma((V, no)), dma((V, no)), dma((V, no)), dma((V, no)),
            dma((V, no)), dma((V, no)), dma((V, no)), dma((V, no)),
            dma((V, n_frame)), dma((V, n_frame)), dma((V, n_frame)), dma((V, n_frame)),
            dma((n_frame,)), dma((n_frame,)), dma((n_frame, no)), dma((n_frame, no)),
            dma((n_frame, no)), dma((n_frame, no)), dma((n_space,)), dma((n_space,)),
            dma((n_frame,)), dma((n_frame,)), dma((4,)), dma((n_frame * w_tout.shape[0] // L,)),
        ],
        compiler_params=pltpu.CompilerParams(
            collective_id=0, has_side_effects=True, vmem_limit_bytes=60 * 1024 * 1024
        ),
        cost_estimate=pl.CostEstimate(
            flops=20_000_000_000, bytes_accessed=300_000_000, transcendentals=3_000_000
        ),
        name="block",
    )(latents, mod, tiles, frames_ok, tokw, w_sqkv, w_sout, w_tqkv, w_tout, target)


def shards(latents, target, timesteps, valid, tile_mask, w_mod, w_sqkv, w_sout, w_tqkv, w_tout):
    videos, frames_dev, span_dev, width = latents.shape
    embed = time_embed(timesteps)
    mod = jnp.dot(embed, w_mod, preferred_element_type=jnp.float32).reshape(videos, 6, width)
    nt = tile_mask.shape[1]
    t_ids = jnp.arange(nt, dtype=jnp.int32)
    tiles = ((tile_mask == 1) & (t_ids[None, None, :] < valid[:, 1][:, None, None])) | (
        t_ids[None, :, None] == t_ids[None, None, :]
    )
    tiles = jnp.pad(tiles.astype(jnp.bfloat16), ((0, 0), (0, PAD - nt), (0, PAD - nt)))
    p_ids = jnp.arange(PAD, dtype=jnp.int32)
    frames_ok = (
        (p_ids[None, None, :] < valid[:, 0][:, None, None])
        | (p_ids[None, :, None] == p_ids[None, None, :])
    ).astype(jnp.bfloat16)
    tile_ids = (lax.axis_index("space") * span_dev + jnp.arange(span_dev, dtype=jnp.int32)) // TILE
    mask = (lax.axis_index("frame") < valid[:, 0][:, None]) & (
        tile_ids[None, :] < valid[:, 1][:, None]
    )
    tokw = jnp.broadcast_to(mask.astype(jnp.float32)[:, :, None], (videos, span_dev, 128))
    shape = (videos, span_dev, width)
    mixed, total, _ = run_kernel(
        latents.reshape(shape), mod, tiles, frames_ok, tokw,
        w_sqkv, w_sout, w_tqkv, w_tout, target.reshape(shape),
    )
    count = jnp.sum(valid[:, 0] * valid[:, 1]).astype(jnp.float32) * TILE
    return (mixed.reshape(latents.shape), total[0, 0] / count)


def solution(mesh):
    return jax.shard_map(
        shards,
        mesh=mesh,
        in_specs=(
            P(None, "frame", "space", None),
            P(None, "frame", "space", None),
            P(),
            P(),
            P(),
            P(),
            P(None, None, "space"),
            P("space", None),
            P(None, None, "frame"),
            P("frame", None),
        ),
        out_specs=(P(None, "frame", "space", None), P()),
        check_vma=False,
    )
```
